32 devices in a mesh: ctx: 8 (over z, y), tp: 4 (over x, core).
Axes of the slice: x: 2, y: 2, z: 4, core: 2. Of those that a mesh axis runs over, the one named last changes fastest.
Arguments:
- resid: bfloat16 [1024, 4096], P('ctx', 'tp'), may hold values from -6 to 6
- query: bfloat16 [1024, 4096], P('ctx', 'tp'), may hold values from -240 to 240
- key: bfloat16 [1024, 1024], P('ctx', 'tp'), may hold values from -8 to 8
- value: bfloat16 [1024, 1024], P('ctx', 'tp'), may hold values from -6 to 6
- router_logit: float32 [1024], P('ctx'), may hold values from -8 to 8
- norm_gain: bfloat16 [4096], P('tp'), may hold values from 0.099609375 to 1.8984375
- w_gate: bfloat16 [4096, 14336], P('tp', 'ctx'), may hold values from -0.09375 to 0.09375
- w_up: bfloat16 [4096, 14336], P('tp', 'ctx'), may hold values from -0.09375 to 0.09375
- w_down: bfloat16 [14336, 4096], P('ctx', 'tp'), may hold values from -0.046875 to 0.046875
- sel_index: int32 [8, 32], P('ctx'), may hold values from 0 to 127, as said below
- sel_count: int32 [8], P('ctx'), may hold values from 1 to 32, 128 in all
Outputs:
- updated: bfloat16 [256, 4096], P('ctx', 'tp')
The draws below stay inside these ranges and needn't reach their ends.
Inputs may be any that keep to these rules, and one draw needn't show every extreme that they name: `sel_index`: each row holds 32 distinct positions within one shard's 128 tokens; the first sel_count entries of row c are that shard's routed tokens, the rest are unused. `sel_count`: the counts sum to 128; some shard holds exactly 32.
All inputs are finite; a program needn't handle non-finite values.
Results may differ from the reference program's by a relative error of at most 0.0044.
Values may be sent and summed in bfloat16 or wider, within the bound.
No kernel may reach another device: no remote copies, remote signals or barrier semaphores. Data moves between devices by JAX's collectives and lax.ppermute only.
A program may use at most 128 MiB of HBM per device.

```python
import math
import jax
import jax.numpy as jnp
import numpy as np
from jax import lax

D = 4096
HEADS = 32
KV_HEADS = 8
HEAD_DIM = 128
FF = 14336
TOK_CTX = 128
CAP = 32
SEQ = 1024
SELECTED = 128
N_CTX = 8


def drawn_rows(key):
    base = jax.random.fold_in(key, 11)
    first, second = jax.random.split(base, 2)
    keys = jax.random.normal(first, (SEQ, KV_HEADS * HEAD_DIM), jnp.float32)
    queries = jax.random.normal(second, (SEQ, HEADS * HEAD_DIM), jnp.float32)
    keys = jnp.clip(keys, -8.0, 8.0)
    return (keys, queries)


def draw_query(key, part):
    keys, queries = drawn_rows(key)
    return queries.astype(jnp.bfloat16)


def draw_key(key, part):
    keys, queries = drawn_rows(key)
    return keys.astype(jnp.bfloat16)


def draw_sel_index(key, part):
    base = jax.random.fold_in(key, 23)
    shard_keys = jax.random.split(base, N_CTX)

    def one_shard(shard_key):
        return jax.random.permutation(shard_key, TOK_CTX)[:CAP].astype(jnp.int32)
    return jax.vmap(one_shard)(shard_keys)


def level_of(key, extent, cuts, least, top_value):
    def one(dim, parts):
        draws = jax.random.uniform(jax.random.fold_in(jax.random.fold_in(key, 6), dim), (parts,), jnp.float32, least / len(cuts), top_value / len(cuts))
        return jnp.repeat(jnp.exp(draws), extent[dim] // parts).reshape((-1,) + (1,) * (len(extent) - dim - 1))

    gain = one(*cuts[0])
    for cut in cuts[1:]:
        gain = gain * one(*cut)
    return gain


def split_up(number_of, total, most, slope):
    loads = [(1 << 20) // math.isqrt(grade ** slope) + 1 for grade in range(2, number_of + 1)]
    surplus, given = total - most - (number_of - 1), [1] * (number_of - 1)
    while surplus > 0:
        candidates = [i for i in range(number_of - 1) if given[i] < most]
        mass, left = sum([loads[i] for i in candidates]), surplus
        for i in candidates:
            more = min(most - given[i], max(1, left * loads[i] // mass), surplus)
            given[i] = given[i] + more
            surplus = surplus - more
    return np.array([most] + given)


def ragged_sizes(key, number_of, total, most, skew):
    if number_of == 2:
        one = jax.random.randint(key, (), max(1, total - most), min(most, total - 1) + 1)
        return jnp.stack([one, total - one])
    lengths = jnp.asarray(split_up(number_of, total, most, skew), jnp.int32)
    couples = (number_of - 1) // 2
    giver, taker = lengths[1:1 + 2 * couples:2], lengths[2:2 + 2 * couples:2]
    room = jnp.minimum(giver - 1, most - taker)
    passed = jax.random.randint(jax.random.fold_in(key, 1), (couples,), 0, 1 << 20) % (room + 1)
    lengths = lengths.at[1:1 + 2 * couples:2].set(giver - passed).at[2:2 + 2 * couples:2].set(taker + passed)
    return lengths[jax.random.permutation(jax.random.fold_in(key, 2), number_of)]


def normal_values(key, shape, scale, limit, cuts=(), held_as=jnp.bfloat16):
    entries = scale * jax.random.normal(key, shape, jnp.float32)
    if cuts:
        entries = entries * level_of(key, shape, cuts, -0.22, 0.18)
    return jnp.clip(entries, -limit, limit).astype(held_as)


def setup_inputs(seed: int = 0) -> dict:
    streams_of = jax.random.split(jax.random.key(seed), 12)
    resid = normal_values(streams_of[0], (SEQ, D), 1.0, 6.0, ((0, 8), (1, 4)))
    query = draw_query(jax.random.fold_in(streams_of[11], 71), 0)
    key = draw_key(jax.random.fold_in(streams_of[11], 71), 0)
    value = normal_values(streams_of[3], (SEQ, KV_HEADS * HEAD_DIM), 1.0, 6.0, ((0, 8), (1, 4)))
    router_logit = normal_values(streams_of[4], (SEQ,), 2.0, 8.0, ((0, 8),), jnp.float32)
    norm_gain = jnp.clip(1.0 + 0.18 * jax.random.normal(streams_of[5], (D,), jnp.float32), 0.099609375, 1.8984375).astype(jnp.bfloat16)
    w_gate = normal_values(streams_of[6], (D, FF), D ** -0.5, 0.09375, ((0, 4), (1, 8)))
    w_up = normal_values(streams_of[7], (D, FF), D ** -0.5, 0.09375, ((0, 4), (1, 8)))
    w_down = normal_values(streams_of[8], (FF, D), FF ** -0.5, 0.046875, ((0, 8), (1, 4)))
    sel_index = draw_sel_index(jax.random.fold_in(streams_of[11], 71), 0)
    sel_count = ragged_sizes(streams_of[10], N_CTX, SELECTED, CAP, 1).astype(jnp.int32)
    return dict(resid=resid, query=query, key=key, value=value, router_logit=router_logit, norm_gain=norm_gain, w_gate=w_gate, w_up=w_up, w_down=w_down, sel_index=sel_index, sel_count=sel_count)


BIG_NEG = -1e+30
EPSILON = 1e-05

def reference(resid, query, key, value, router_logit, norm_gain, w_gate, w_up, w_down, sel_index, sel_count):
    slot = jnp.arange(CAP, dtype=jnp.int32)
    live = (slot[None, :] < sel_count[:, None]).reshape(-1)
    position = (jnp.arange(N_CTX, dtype=jnp.int32)[:, None] * TOK_CTX + sel_index).reshape(-1).astype(jnp.int32)
    key_pos = jnp.where(live, position, SEQ)
    rows_x = resid[position]
    slots = rows_x.shape[0]
    group = HEADS // KV_HEADS
    scale = HEAD_DIM ** (-0.5)
    q_heads = query[position].reshape(slots, HEADS, HEAD_DIM).transpose(1, 0, 2)
    k_heads = jnp.repeat(key[position].reshape(slots, KV_HEADS, HEAD_DIM).transpose(1, 0, 2), group, axis=0)
    v_heads = jnp.repeat(value[position].reshape(slots, KV_HEADS, HEAD_DIM).transpose(1, 0, 2), group, axis=0)
    allowed = key_pos[None, :] <= position[:, None]

    def one_head(operands):
        q_one, k_one, v_one = operands
        scores = jnp.dot(q_one, k_one.T, preferred_element_type=jnp.float32) * scale
        scores = jnp.where(allowed, scores, BIG_NEG)
        top = lax.optimization_barrier(jnp.max(scores, axis=1, keepdims=True))
        prob = jnp.exp(scores - top)
        total = lax.optimization_barrier(jnp.sum(prob, axis=1, keepdims=True))
        return jnp.dot(prob.astype(jnp.bfloat16), v_one, preferred_element_type=jnp.float32) / total
    head_out = lax.map(one_head, (q_heads, k_heads, v_heads))
    attn = head_out.transpose(1, 0, 2).reshape(slots, D)
    rows_float = rows_x.astype(jnp.float32)
    h_one = (rows_float + attn).astype(jnp.bfloat16)
    h_float = h_one.astype(jnp.float32)
    rscale = lax.rsqrt(lax.optimization_barrier(jnp.mean(h_float * h_float, axis=1)) + EPSILON)
    scaled = (h_float * norm_gain.astype(jnp.float32)[None, :]).astype(jnp.bfloat16)
    gate = rscale[:, None] * jnp.dot(scaled, w_gate, preferred_element_type=jnp.float32)
    up_val = rscale[:, None] * jnp.dot(scaled, w_up, preferred_element_type=jnp.float32)
    hidden = (jax.nn.silu(gate) * up_val).astype(jnp.bfloat16)
    mlp = jnp.dot(hidden, w_down, preferred_element_type=jnp.float32).astype(jnp.bfloat16)
    router = jax.nn.sigmoid(router_logit[position])
    result = rows_float + router[:, None] * (attn + mlp.astype(jnp.float32))
    return jnp.where(live[:, None], result, 0.0).astype(jnp.bfloat16)
```

```python
import functools

import jax
import jax.numpy as jnp
from jax import lax
from jax.experimental import pallas as pl
from jax.experimental.pallas import tpu as pltpu
from jax.sharding import PartitionSpec as P

D = 4096
HEAD_DIM = 128
CAP = 32


BIG_NEG = -1e30
EPSILON = 1e-05


def swapped(value, axis, distance):
    mask = 2**distance
    pairs = [(source, source ^ mask) for source in range(lax.axis_size(axis))]
    return lax.ppermute(value, axis, pairs)


def masked_scores(queries, keys, key_pos, query_pos, scale):
    scores = jnp.einsum("qkgd,skd->kgqs", queries, keys, preferred_element_type=jnp.float32) * scale
    allowed = key_pos[None, :] <= query_pos[:, None]
    return jnp.where(allowed[None, None], scores, BIG_NEG)


def pick_bit(shard_index, bit):
    return shard_index // (1 << bit) % 2


def ordered(own_piece, partner_piece, my_bit, along):
    lower_part = jnp.where(my_bit == 0, own_piece, partner_piece)
    upper_part = jnp.where(my_bit == 0, partner_piece, own_piece)
    return jnp.concatenate([lower_part, upper_part], axis=along)


def route_members(blocks, low_bits, my_shard, mover):
    per_dest = blocks.shape[1]
    width = blocks.shape[2]
    blocks_now = blocks.reshape((2,) * low_bits + (per_dest, width))
    for bit in range(low_bits):
        my_bit = pick_bit(my_shard, bit)
        retained = lax.dynamic_index_in_dim(blocks_now, my_bit, low_bits - 1, keepdims=False)
        outgoing = lax.dynamic_index_in_dim(blocks_now, 1 - my_bit, low_bits - 1, keepdims=False)
        arrived = mover(outgoing, bit)
        lower_part = jnp.where(my_bit == 0, retained, arrived)
        upper_part = jnp.where(my_bit == 0, arrived, retained)
        blocks_now = jnp.stack([lower_part, upper_part], axis=0)
    return blocks_now.reshape(blocks.shape)


def local_exchange(
    resid, query, key, value, router_logit, norm_gain, w_gate, w_up, w_down, sel_index, sel_count
):
    shards = lax.axis_size("ctx")
    my_shard = lax.axis_index("ctx")
    tok_ctx = resid.shape[0]
    width = resid.shape[1]
    kv_local = key.shape[1] // HEAD_DIM
    group = query.shape[1] // key.shape[1]
    scale = HEAD_DIM ** (-0.5)
    index = sel_index[0]
    count = sel_count[0]
    slot = jnp.arange(CAP, dtype=jnp.int32)
    live = slot < count
    query_pos = my_shard * tok_ctx + index
    key_pos = jnp.where(live, query_pos, tok_ctx * shards)
    rows_x = jnp.take(resid, index, axis=0)
    q_rows = jnp.take(query, index, axis=0).reshape(CAP, kv_local, group, HEAD_DIM)
    k_rows = jnp.take(key, index, axis=0)
    v_rows = jnp.take(value, index, axis=0)
    router = jax.nn.sigmoid(jnp.take(router_logit, index, axis=0))
    all_k, all_v, all_pos = (
        lax.all_gather(k_rows, "ctx", axis=0, tiled=True),
        lax.all_gather(v_rows, "ctx", axis=0, tiled=True),
        lax.all_gather(key_pos, "ctx", axis=0, tiled=True),
    )
    scores = masked_scores(q_rows, all_k.reshape(-1, kv_local, HEAD_DIM), all_pos, query_pos, scale)
    top = jnp.max(scores, axis=-1, keepdims=True)
    prob = jnp.exp(scores - top)
    total = jnp.sum(prob, axis=-1)
    mixed = jnp.einsum(
        "kgqs,skd->kgqd",
        prob.astype(jnp.bfloat16),
        all_v.reshape(-1, kv_local, HEAD_DIM),
        preferred_element_type=jnp.float32,
    )
    mixed = mixed / total[..., None]
    attn = mixed.transpose(2, 0, 1, 3).reshape(CAP, width)
    rows_float = rows_x.astype(jnp.float32)
    h_one = (rows_float + attn).astype(jnp.bfloat16)
    low_bits = 2
    members = 1 << low_bits
    high_bits = shards.bit_length() - 1 - low_bits
    per_dest = CAP // members
    weight_pair = jnp.stack([w_gate, w_up], axis=0)
    down_block = w_down
    for bit in range(low_bits):
        my_bit = pick_bit(my_shard, bit)
        weight_pair = ordered(weight_pair, swapped(weight_pair, "ctx", bit), my_bit, 2)
        down_block = ordered(down_block, swapped(down_block, "ctx", bit), my_bit, 0)

    def send_rows(piece, bit):
        return swapped(piece, "ctx", bit)

    def send_back(piece, bit):
        return swapped(piece, "ctx", bit)

    routed = route_members(h_one.reshape(members, per_dest, width), low_bits, my_shard, send_rows)
    spread = routed.reshape(members * per_dest, width)
    for step in range(high_bits):
        bit = low_bits + step
        spread = ordered(spread, swapped(spread, "ctx", bit), pick_bit(my_shard, bit), 0)
    compact_float = spread.astype(jnp.float32)
    square_part = jnp.sum(compact_float * compact_float, axis=1)
    scaled = (compact_float * norm_gain.astype(jnp.float32)[None, :]).astype(jnp.bfloat16)
    gate_part = jnp.dot(scaled, weight_pair[0], preferred_element_type=jnp.float32)
    up_part = jnp.dot(scaled, weight_pair[1], preferred_element_type=jnp.float32)
    gate_sum, up_sum, square_sum = lax.psum((gate_part, up_part, square_part), "tp")
    rscale = lax.rsqrt(square_sum / D + EPSILON)
    hidden = (jax.nn.silu(rscale[:, None] * gate_sum) * (rscale[:, None] * up_sum)).astype(
        jnp.bfloat16
    )
    partial_value = jnp.dot(hidden, down_block, preferred_element_type=jnp.float32)
    partial_value = partial_value.reshape(1 << high_bits, members * per_dest, width)
    for step in reversed(range(high_bits)):
        bit = low_bits + step
        my_bit = pick_bit(my_shard, bit)
        halves = partial_value.reshape(2, partial_value.shape[0] // 2, members * per_dest, width)
        retained = lax.dynamic_index_in_dim(halves, my_bit, 0, keepdims=False)
        outgoing = lax.dynamic_index_in_dim(halves, 1 - my_bit, 0, keepdims=False)
        partial_value = retained + swapped(outgoing, "ctx", bit)
    mlp_rows = partial_value[0].astype(jnp.bfloat16).reshape(members, per_dest, width)
    mine = route_members(mlp_rows, low_bits, my_shard, send_back).reshape(CAP, width)
    result = rows_float + router[:, None] * (attn + mine.astype(jnp.float32))
    return jnp.where(live[:, None], result, 0.0).astype(jnp.bfloat16)


LANES = 128
ROWS = 32


def fits(shards, tps, tok_ctx, width, kv_width, hidden_width):
    return (
        shards == 8
        and tps == 4
        and tok_ctx % LANES == 0
        and width % LANES == 0
        and kv_width % HEAD_DIM == 0
        and hidden_width % 256 == 0
    )


def block_shard(block, my_shard):
    return my_shard ^ (((block & 3) << 1) | (block >> 2))


def column_of(row, size):
    down = lax.broadcasted_iota(jnp.int32, (size, size), 0)
    across = lax.broadcasted_iota(jnp.int32, (size, size), 1)
    return jnp.sum(jnp.where(down == across, row, jnp.zeros_like(row)), axis=1, keepdims=True)


def row_of(column, size):
    down = lax.broadcasted_iota(jnp.int32, (size, size), 0)
    across = lax.broadcasted_iota(jnp.int32, (size, size), 1)
    return jnp.sum(jnp.where(down == across, column, jnp.zeros_like(column)), axis=0, keepdims=True)


def gather_kernel(count_ref, index_ref, resid_ref, query_ref, key_ref, value_ref, kv_ref, x_ref, q_ref):
    tok_ctx = resid_ref.shape[0]
    kv_width = key_ref.shape[1]
    index = column_of(index_ref[...], CAP)
    chosen = lax.broadcasted_iota(jnp.int32, (CAP, tok_ctx), 1) == index
    pick = chosen.astype(jnp.bfloat16)

    def take(ref):
        return jnp.dot(pick, ref[...], preferred_element_type=jnp.float32).astype(jnp.bfloat16)

    kv_ref[:, :kv_width] = take(key_ref)
    kv_ref[:, kv_width : 2 * kv_width] = take(value_ref)
    lane = lax.broadcasted_iota(jnp.int32, (CAP, LANES), 1)
    slot = lax.broadcasted_iota(jnp.int32, (CAP, LANES), 0)
    live = (slot < count_ref[0]).astype(jnp.int32)
    note = jnp.where(lane < 32, index % LANES, jnp.where(lane < 64, index // LANES, live))
    kv_ref[:, 2 * kv_width :] = note.astype(jnp.float32).astype(jnp.bfloat16)
    x_ref[...] = take(resid_ref)
    q_ref[...] = take(query_ref)


def attention_kernel(place_ref, index_ref, kv_ref, q_ref, x_ref, h_ref, attn_ref, *, tok_ctx):
    my_shard = place_ref[0]
    slots = kv_ref.shape[0]
    kv_width = (kv_ref.shape[1] - LANES) // 2
    kv_heads = kv_width // HEAD_DIM
    group = q_ref.shape[1] // kv_width
    scale = HEAD_DIM ** (-0.5)
    low = kv_ref[:, 2 * kv_width : 2 * kv_width + 1].astype(jnp.float32)
    high = kv_ref[:, 2 * kv_width + 32 : 2 * kv_width + 33].astype(jnp.float32)
    live = kv_ref[:, 2 * kv_width + 64 : 2 * kv_width + 65].astype(jnp.float32)
    block = lax.broadcasted_iota(jnp.int32, (slots, 1), 0) // CAP
    start = (block_shard(block, my_shard) * tok_ctx).astype(jnp.float32)
    end = float(tok_ctx * (slots // CAP))
    key_pos = jnp.where(live > 0.5, start + high * LANES + low, end)
    key_row = row_of(key_pos, slots)
    index = column_of(index_ref[...], CAP)
    query_pos = (index + my_shard * tok_ctx).astype(jnp.float32)
    allowed = jnp.concatenate([key_row <= query_pos] * group, axis=0)
    for head in range(kv_heads):
        keys = kv_ref[:, head * HEAD_DIM : (head + 1) * HEAD_DIM]
        values = kv_ref[:, kv_width + head * HEAD_DIM : kv_width + (head + 1) * HEAD_DIM]
        base = head * group * HEAD_DIM
        queries = jnp.concatenate(
            [q_ref[:, base + g * HEAD_DIM : base + (g + 1) * HEAD_DIM] for g in range(group)], axis=0
        )
        scores = (
            lax.dot_general(queries, keys, (((1,), (1,)), ((), ())), preferred_element_type=jnp.float32)
            * scale
        )
        scores = jnp.where(allowed, scores, BIG_NEG)
        top = jnp.max(scores, axis=1, keepdims=True)
        prob = jnp.exp(scores - top)
        total = jnp.sum(prob, axis=1, keepdims=True)
        mixed = jnp.dot(prob.astype(jnp.bfloat16), values, preferred_element_type=jnp.float32) / total
        for g in range(group):
            columns = slice(base + g * HEAD_DIM, base + (g + 1) * HEAD_DIM)
            piece = mixed[g * CAP : (g + 1) * CAP]
            attn_ref[:, columns] = piece
            h_ref[:, columns] = (x_ref[:, columns].astype(jnp.float32) + piece).astype(jnp.bfloat16)


def select_kernel(place_ref, kv_ref, pack_ref, spread_ref):
    slots = kv_ref.shape[0]
    packed = pack_ref.shape[0]
    my_shard = place_ref[0]
    my_tp = place_ref[1]
    lane0 = kv_ref.shape[1] - 64
    live = kv_ref[:, lane0 : lane0 + 1].astype(jnp.float32)
    down = lax.broadcasted_iota(jnp.int32, (slots, slots), 0)
    across = lax.broadcasted_iota(jnp.int32, (slots, slots), 1)

    def order(slot):
        return block_shard(slot // CAP, my_shard) * CAP + slot % CAP

    live_row = row_of(live, slots)
    before = (order(across) < order(down)).astype(jnp.float32)
    place = jnp.sum(before * live_row, axis=1, keepdims=True).astype(jnp.int32)
    quarter = place // ROWS
    relative = quarter ^ my_tp
    swapped_bits = ((relative & 1) << 1) | (relative >> 1)
    spot = jnp.where(live > 0.5, swapped_bits * ROWS + place % ROWS, packed).astype(jnp.float32)
    spot_row = row_of(spot, slots)
    spread_ref[...] = (
        lax.broadcasted_iota(jnp.int32, (slots, packed), 1).astype(jnp.float32) == spot
    ).astype(jnp.bfloat16)
    pack_ref[...] = (
        lax.broadcasted_iota(jnp.int32, (packed, slots), 0).astype(jnp.float32) == spot_row
    ).astype(jnp.bfloat16)


def expand_kernel(pack_ref, rows_ref, gain_ref, gate_ref, up_ref, out_ref, scaled_ref):
    step = pl.program_id(0)
    hidden_width = (out_ref.shape[1] - LANES) // 2
    tile = gate_ref.shape[1]

    @pl.when(step == 0)
    def _():
        rows = jnp.dot(pack_ref[...], rows_ref[...], preferred_element_type=jnp.float32)
        scaled_ref[...] = (rows * gain_ref[...].astype(jnp.float32)).astype(jnp.bfloat16)
        square = jnp.sum(rows * rows, axis=1, keepdims=True)
        coarse = square.astype(jnp.bfloat16).astype(jnp.float32)
        fine = square - coarse
        lane = lax.broadcasted_iota(jnp.int32, (rows.shape[0], LANES), 1)
        out_ref[:, 2 * hidden_width :] = jnp.where(lane < 64, coarse, fine).astype(jnp.bfloat16)

    scaled = scaled_ref[...]
    at = pl.multiple_of(step * tile, tile)
    out_ref[:, pl.ds(at, tile)] = jnp.dot(
        scaled, gate_ref[...], preferred_element_type=jnp.float32
    ).astype(jnp.bfloat16)
    out_ref[:, pl.ds(hidden_width + at, tile)] = jnp.dot(
        scaled, up_ref[...], preferred_element_type=jnp.float32
    ).astype(jnp.bfloat16)


def hidden_kernel(mine_ref, other_ref, out_ref):
    hidden_width = out_ref.shape[1]
    square = mine_ref[:, 2 * hidden_width :].astype(jnp.float32) + other_ref[
        :, 2 * hidden_width :
    ].astype(jnp.float32)
    rscale = lax.rsqrt((square[:, :1] + square[:, 64:65]) / D + EPSILON)
    gate = rscale * (
        mine_ref[:, :hidden_width].astype(jnp.float32) + other_ref[:, :hidden_width].astype(jnp.float32)
    )
    up = rscale * (
        mine_ref[:, hidden_width : 2 * hidden_width].astype(jnp.float32)
        + other_ref[:, hidden_width : 2 * hidden_width].astype(jnp.float32)
    )
    out_ref[...] = (gate / (1.0 + jnp.exp(-gate)) * up).astype(jnp.bfloat16)


def down_kernel(hidden_ref, down_ref, spread_ref, out_ref):
    part = jnp.dot(hidden_ref[...], down_ref[...], preferred_element_type=jnp.float32)
    out_ref[...] = jnp.dot(
        spread_ref[...], part.astype(jnp.bfloat16), preferred_element_type=jnp.float32
    ).astype(jnp.bfloat16)


def finish_kernel(count_ref, index_ref, logit_ref, x_ref, attn_ref, a_ref, b_ref, c_ref, d_ref, out_ref):
    tok_ctx = logit_ref.shape[1]
    index = column_of(index_ref[...], CAP)
    chosen = lax.broadcasted_iota(jnp.int32, (CAP, tok_ctx), 1) == index
    logit = jnp.sum(jnp.where(chosen, logit_ref[...], 0.0), axis=1, keepdims=True)
    router = 1.0 / (1.0 + jnp.exp(-logit))
    mlp = a_ref[...].astype(jnp.float32) + b_ref[...].astype(jnp.float32)
    mlp = mlp + (c_ref[...].astype(jnp.float32) + d_ref[...].astype(jnp.float32))
    mlp = mlp.astype(jnp.bfloat16).astype(jnp.float32)
    result = x_ref[...].astype(jnp.float32) + router * (attn_ref[...] + mlp)
    live = lax.broadcasted_iota(jnp.int32, (CAP, 1), 0) < count_ref[0]
    out_ref[...] = jnp.where(live, result, 0.0).astype(jnp.bfloat16)


def swap(value, axis, mask):
    pairs = [(source, source ^ mask) for source in range(lax.axis_size(axis))]
    return lax.ppermute(value, axis, pairs)


def gathered(piece):
    for mask in (2, 4, 1):
        piece = jnp.concatenate([piece, swap(piece, "ctx", mask)], axis=0)
    return piece


def local(
    resid, query, key, value, router_logit, norm_gain, w_gate, w_up, w_down, sel_index, sel_count
):
    shards = lax.axis_size("ctx")
    tps = lax.axis_size("tp")
    tok_ctx, width = resid.shape
    kv_width = key.shape[1]
    hidden_width = w_gate.shape[1]
    if not fits(shards, tps, tok_ctx, width, kv_width, hidden_width):
        return local_exchange(
            resid, query, key, value, router_logit, norm_gain, w_gate, w_up, w_down, sel_index, sel_count
        )
    slots = shards * CAP
    packed = slots // 2
    bf16 = jnp.bfloat16
    shape = jax.ShapeDtypeStruct
    smem = pl.BlockSpec(memory_space=pltpu.SMEM)
    vmem = pl.BlockSpec(memory_space=pltpu.VMEM)
    place = jnp.stack([lax.axis_index("ctx"), lax.axis_index("tp")]).astype(jnp.int32)

    kv, rows_x, q_rows = pl.pallas_call(
        gather_kernel,
        out_shape=(
            shape((CAP, 2 * kv_width + LANES), bf16),
            shape((CAP, width), bf16),
            shape((CAP, width), bf16),
        ),
        in_specs=[smem] + [vmem] * 5,
        out_specs=(vmem,) * 3,
        name="gather_rows",
    )(sel_count, sel_index, resid, query, key, value)
    all_kv = gathered(kv)
    h_one, attn = pl.pallas_call(
        functools.partial(attention_kernel, tok_ctx=tok_ctx),
        out_shape=(shape((CAP, width), bf16), shape((CAP, width), jnp.float32)),
        in_specs=[smem] + [vmem] * 4,
        out_specs=(vmem,) * 2,
        name="attention",
    )(place, sel_index, all_kv, q_rows, rows_x)
    pack, spread = pl.pallas_call(
        select_kernel,
        out_shape=(shape((packed, slots), bf16), shape((slots, packed), bf16)),
        in_specs=[smem, vmem],
        out_specs=(vmem,) * 2,
        name="select",
    )(place, all_kv)
    rows = gathered(h_one)
    tile = 256
    part = pl.pallas_call(
        expand_kernel,
        out_shape=shape((packed, 2 * hidden_width + LANES), bf16),
        grid=(hidden_width // tile,),
        in_specs=[
            pl.BlockSpec((packed, slots), lambda j: (0, 0)),
            pl.BlockSpec((slots, width), lambda j: (0, 0)),
            pl.BlockSpec((1, width), lambda j: (0, 0)),
            pl.BlockSpec((width, tile), lambda j: (0, j)),
            pl.BlockSpec((width, tile), lambda j: (0, j)),
        ],
        out_specs=pl.BlockSpec((packed, 2 * hidden_width + LANES), lambda j: (0, 0)),
        scratch_shapes=[pltpu.VMEM((packed, width), bf16)],
        name="expand",
    )(pack, rows, norm_gain.reshape(1, width), w_gate, w_up)
    half = packed // 2
    quarter = packed // 4
    summed = (
        part[:half].astype(jnp.float32) + swap(part[half:], "tp", 1).astype(jnp.float32)
    ).astype(bf16)
    other = swap(summed[quarter:], "tp", 2)
    hidden = pl.pallas_call(
        hidden_kernel,
        out_shape=shape((quarter, hidden_width), bf16),
        in_specs=[vmem] * 2,
        out_specs=vmem,
        name="hidden",
    )(summed[:quarter], other)
    hidden = jnp.concatenate([hidden, swap(hidden, "tp", 2)], axis=0)
    hidden = jnp.concatenate([hidden, swap(hidden, "tp", 1)], axis=0)
    partial_value = pl.pallas_call(
        down_kernel,
        out_shape=shape((slots, width), bf16),
        grid=(width // tile,),
        in_specs=[
            pl.BlockSpec((packed, hidden_width), lambda j: (0, 0)),
            pl.BlockSpec((hidden_width, tile), lambda j: (0, j)),
            pl.BlockSpec((slots, packed), lambda j: (0, 0)),
        ],
        out_specs=pl.BlockSpec((slots, tile), lambda j: (0, j)),
        name="down",
    )(hidden, w_down, spread)
    half = slots // 2
    sums = (
        partial_value[:half].astype(jnp.float32)
        + swap(partial_value[half:], "ctx", 1).astype(jnp.float32)
    ).astype(bf16)
    pieces = [sums[:CAP]] + [
        swap(sums[b * CAP : (b + 1) * CAP], "ctx", 2 * b) for b in range(1, 4)
    ]
    return pl.pallas_call(
        finish_kernel,
        out_shape=shape((CAP, width), bf16),
        in_specs=[smem] + [vmem] * 8,
        out_specs=vmem,
        name="finish",
    )(sel_count, sel_index, router_logit.reshape(1, tok_ctx), rows_x, attn, *pieces)


def solution(mesh):
    in_specs = (
        P("ctx", "tp"),
        P("ctx", "tp"),
        P("ctx", "tp"),
        P("ctx", "tp"),
        P("ctx"),
        P("tp"),
        P("tp", "ctx"),
        P("tp", "ctx"),
        P("ctx", "tp"),
        P("ctx", None),
        P("ctx"),
    )
    out_specs = P("ctx", "tp")
    return jax.shard_map(local, mesh=mesh, in_specs=in_specs, out_specs=out_specs, check_vma=False)
```

```python
import functools

import jax
import jax.numpy as jnp
from jax import lax
from jax.experimental import pallas as pl
from jax.experimental.pallas import tpu as pltpu
from jax.sharding import PartitionSpec as P

D = 4096
HEAD_DIM = 128
CAP = 32


BIG_NEG = -1e30
EPSILON = 1e-05


def swapped(value, axis, distance):
    mask = 2**distance
    pairs = [(source, source ^ mask) for source in range(lax.axis_size(axis))]
    return lax.ppermute(value, axis, pairs)


def masked_scores(queries, keys, key_pos, query_pos, scale):
    scores = jnp.einsum("qkgd,skd->kgqs", queries, keys, preferred_element_type=jnp.float32) * scale
    allowed = key_pos[None, :] <= query_pos[:, None]
    return jnp.where(allowed[None, None], scores, BIG_NEG)


def pick_bit(shard_index, bit):
    return shard_index // (1 << bit) % 2


def ordered(own_piece, partner_piece, my_bit, along):
    lower_part = jnp.where(my_bit == 0, own_piece, partner_piece)
    upper_part = jnp.where(my_bit == 0, partner_piece, own_piece)
    return jnp.concatenate([lower_part, upper_part], axis=along)


def route_members(blocks, low_bits, my_shard, mover):
    per_dest = blocks.shape[1]
    width = blocks.shape[2]
    blocks_now = blocks.reshape((2,) * low_bits + (per_dest, width))
    for bit in range(low_bits):
        my_bit = pick_bit(my_shard, bit)
        retained = lax.dynamic_index_in_dim(blocks_now, my_bit, low_bits - 1, keepdims=False)
        outgoing = lax.dynamic_index_in_dim(blocks_now, 1 - my_bit, low_bits - 1, keepdims=False)
        arrived = mover(outgoing, bit)
        lower_part = jnp.where(my_bit == 0, retained, arrived)
        upper_part = jnp.where(my_bit == 0, arrived, retained)
        blocks_now = jnp.stack([lower_part, upper_part], axis=0)
    return blocks_now.reshape(blocks.shape)


def local_exchange(
    resid, query, key, value, router_logit, norm_gain, w_gate, w_up, w_down, sel_index, sel_count
):
    shards = lax.axis_size("ctx")
    my_shard = lax.axis_index("ctx")
    tok_ctx = resid.shape[0]
    width = resid.shape[1]
    kv_local = key.shape[1] // HEAD_DIM
    group = query.shape[1] // key.shape[1]
    scale = HEAD_DIM ** (-0.5)
    index = sel_index[0]
    count = sel_count[0]
    slot = jnp.arange(CAP, dtype=jnp.int32)
    live = slot < count
    query_pos = my_shard * tok_ctx + index
    key_pos = jnp.where(live, query_pos, tok_ctx * shards)
    rows_x = jnp.take(resid, index, axis=0)
    q_rows = jnp.take(query, index, axis=0).reshape(CAP, kv_local, group, HEAD_DIM)
    k_rows = jnp.take(key, index, axis=0)
    v_rows = jnp.take(value, index, axis=0)
    router = jax.nn.sigmoid(jnp.take(router_logit, index, axis=0))
    all_k, all_v, all_pos = (
        lax.all_gather(k_rows, "ctx", axis=0, tiled=True),
        lax.all_gather(v_rows, "ctx", axis=0, tiled=True),
        lax.all_gather(key_pos, "ctx", axis=0, tiled=True),
    )
    scores = masked_scores(q_rows, all_k.reshape(-1, kv_local, HEAD_DIM), all_pos, query_pos, scale)
    top = jnp.max(scores, axis=-1, keepdims=True)
    prob = jnp.exp(scores - top)
    total = jnp.sum(prob, axis=-1)
    mixed = jnp.einsum(
        "kgqs,skd->kgqd",
        prob.astype(jnp.bfloat16),
        all_v.reshape(-1, kv_local, HEAD_DIM),
        preferred_element_type=jnp.float32,
    )
    mixed = mixed / total[..., None]
    attn = mixed.transpose(2, 0, 1, 3).reshape(CAP, width)
    rows_float = rows_x.astype(jnp.float32)
    h_one = (rows_float + attn).astype(jnp.bfloat16)
    low_bits = 2
    members = 1 << low_bits
    high_bits = shards.bit_length() - 1 - low_bits
    per_dest = CAP // members
    weight_pair = jnp.stack([w_gate, w_up], axis=0)
    down_block = w_down
    for bit in range(low_bits):
        my_bit = pick_bit(my_shard, bit)
        weight_pair = ordered(weight_pair, swapped(weight_pair, "ctx", bit), my_bit, 2)
        down_block = ordered(down_block, swapped(down_block, "ctx", bit), my_bit, 0)

    def send_rows(piece, bit):
        return swapped(piece, "ctx", bit)

    def send_back(piece, bit):
        return swapped(piece, "ctx", bit)

    routed = route_members(h_one.reshape(members, per_dest, width), low_bits, my_shard, send_rows)
    spread = routed.reshape(members * per_dest, width)
    for step in range(high_bits):
        bit = low_bits + step
        spread = ordered(spread, swapped(spread, "ctx", bit), pick_bit(my_shard, bit), 0)
    compact_float = spread.astype(jnp.float32)
    square_part = jnp.sum(compact_float * compact_float, axis=1)
    scaled = (compact_float * norm_gain.astype(jnp.float32)[None, :]).astype(jnp.bfloat16)
    gate_part = jnp.dot(scaled, weight_pair[0], preferred_element_type=jnp.float32)
    up_part = jnp.dot(scaled, weight_pair[1], preferred_element_type=jnp.float32)
    gate_sum, up_sum, square_sum = lax.psum((gate_part, up_part, square_part), "tp")
    rscale = lax.rsqrt(square_sum / D + EPSILON)
    hidden = (jax.nn.silu(rscale[:, None] * gate_sum) * (rscale[:, None] * up_sum)).astype(
        jnp.bfloat16
    )
    partial_value = jnp.dot(hidden, down_block, preferred_element_type=jnp.float32)
    partial_value = partial_value.reshape(1 << high_bits, members * per_dest, width)
    for step in reversed(range(high_bits)):
        bit = low_bits + step
        my_bit = pick_bit(my_shard, bit)
        halves = partial_value.reshape(2, partial_value.shape[0] // 2, members * per_dest, width)
        retained = lax.dynamic_index_in_dim(halves, my_bit, 0, keepdims=False)
        outgoing = lax.dynamic_index_in_dim(halves, 1 - my_bit, 0, keepdims=False)
        partial_value = retained + swapped(outgoing, "ctx", bit)
    mlp_rows = partial_value[0].astype(jnp.bfloat16).reshape(members, per_dest, width)
    mine = route_members(mlp_rows, low_bits, my_shard, send_back).reshape(CAP, width)
    result = rows_float + router[:, None] * (attn + mine.astype(jnp.float32))
    return jnp.where(live[:, None], result, 0.0).astype(jnp.bfloat16)


LANES = 128
ROWS = 32


def fits(shards, tps, tok_ctx, width, kv_width, hidden_width):
    return (
        shards == 8
        and tps == 4
        and tok_ctx % LANES == 0
        and width % LANES == 0
        and kv_width % HEAD_DIM == 0
        and hidden_width % 256 == 0
    )


def block_shard(block, my_shard):
    return my_shard ^ (((block & 3) << 1) | (block >> 2))


def column_of(row, size):
    down = lax.broadcasted_iota(jnp.int32, (size, size), 0)
    across = lax.broadcasted_iota(jnp.int32, (size, size), 1)
    return jnp.sum(jnp.where(down == across, row, jnp.zeros_like(row)), axis=1, keepdims=True)


def row_of(column, size):
    down = lax.broadcasted_iota(jnp.int32, (size, size), 0)
    across = lax.broadcasted_iota(jnp.int32, (size, size), 1)
    return jnp.sum(jnp.where(down == across, column, jnp.zeros_like(column)), axis=0, keepdims=True)


def gather_kernel(
    count_ref,
    index_hbm,
    logit_hbm,
    resid_hbm,
    query_hbm,
    key_hbm,
    value_hbm,
    load_ref,
    router_ref,
    index_ref,
    logit_ref,
    resid_ref,
    query_ref,
    key_ref,
    value_ref,
    sems,
):
    sources = (index_hbm, key_hbm, value_hbm, resid_hbm, query_hbm, logit_hbm)
    places = (index_ref, key_ref, value_ref, resid_ref, query_ref, logit_ref)
    copies = [
        pltpu.make_async_copy(source, target, sems.at[at])
        for at, (source, target) in enumerate(zip(sources, places))
    ]
    for copy in copies:
        copy.start()
    tok_ctx = resid_ref.shape[0]
    kv_width = key_ref.shape[1]
    width = resid_ref.shape[1]
    copies[0].wait()
    index = column_of(index_ref[...], CAP)
    chosen = lax.broadcasted_iota(jnp.int32, (CAP, tok_ctx), 1) == index
    pick = chosen.astype(jnp.bfloat16)

    def take(at, base):
        copies[at].wait()
        rows = jnp.dot(pick, places[at][...], preferred_element_type=jnp.float32)
        load_ref[:, base : base + rows.shape[1]] = rows.astype(jnp.bfloat16)

    lane = lax.broadcasted_iota(jnp.int32, (CAP, LANES), 1)
    live = (lax.broadcasted_iota(jnp.int32, (CAP, LANES), 0) < count_ref[0]).astype(jnp.int32)
    note = jnp.where(lane < 32, index % LANES, jnp.where(lane < 64, index // LANES, live))
    load_ref[:, :LANES] = note.astype(jnp.float32).astype(jnp.bfloat16)
    take(1, LANES)
    take(2, LANES + kv_width)
    take(3, LANES + 2 * kv_width)
    take(4, LANES + 2 * kv_width + width)
    copies[5].wait()
    logit = jnp.sum(jnp.where(chosen, logit_ref[...], 0.0), axis=1, keepdims=True)
    router = 1.0 / (1.0 + jnp.exp(-logit))
    router_ref[...] = jnp.where(lane < 64, router, live.astype(jnp.float32))


def mix_kernel(place_ref, *refs):
    loads = refs[:8]
    gain_ref, gate_ref, up_ref, keep_ref, send_ref, attn_ref, spread_ref = refs[8:]
    my_shard = place_ref[0]
    my_tp = place_ref[1]
    slots = 8 * CAP
    packed = 2 * keep_ref.shape[0]
    hidden_width = gate_ref.shape[1]
    width = gate_ref.shape[0]
    kv_width = (loads[0].shape[1] - LANES - 2 * width) // 2
    kv_heads = kv_width // HEAD_DIM
    group = width // kv_width
    scale = HEAD_DIM ** (-0.5)

    notes = jnp.concatenate([ref[:, :LANES] for ref in loads], axis=0).astype(jnp.float32)
    live = notes[:, 64:65]
    down = lax.broadcasted_iota(jnp.int32, (slots, slots), 0)
    across = lax.broadcasted_iota(jnp.int32, (slots, slots), 1)

    def order(slot):
        return block_shard(slot // CAP, my_shard) * CAP + slot % CAP

    before = (order(across) < order(down)).astype(jnp.float32)
    place = jnp.sum(before * row_of(live, slots), axis=1, keepdims=True).astype(jnp.int32)
    relative = (place // ROWS) ^ my_tp
    swapped_bits = ((relative & 1) << 1) | (relative >> 1)
    spot = jnp.where(live > 0.5, swapped_bits * ROWS + place % ROWS, packed).astype(jnp.float32)
    spread_ref[...] = (
        lax.broadcasted_iota(jnp.int32, (slots, packed), 1).astype(jnp.float32) == spot
    ).astype(jnp.bfloat16)
    hit = lax.broadcasted_iota(jnp.int32, (packed, slots), 0).astype(jnp.float32) == row_of(spot, slots)
    pack = hit.astype(jnp.bfloat16)
    slot = lax.broadcasted_iota(jnp.int32, (slots, 1), 0)
    tok_ctx = place_ref[2]
    position = (
        block_shard(slot // CAP, my_shard) * tok_ctx
        + notes[:, :1].astype(jnp.int32)
        + LANES * notes[:, 32:33].astype(jnp.int32)
    ).astype(jnp.float32)
    position = jnp.sum(jnp.where(hit, row_of(position, slots), 0.0), axis=1, keepdims=True)
    allowed = row_of(position, packed) <= position
    allowed = jnp.concatenate([allowed] * group, axis=0)

    def packed_columns(base, size):
        rows = jnp.concatenate([ref[:, base : base + size] for ref in loads], axis=0)
        return jnp.dot(pack, rows, preferred_element_type=jnp.float32)

    q_base = LANES + 2 * kv_width + width
    x_base = LANES + 2 * kv_width
    for head in range(kv_heads):
        keys = packed_columns(LANES + head * HEAD_DIM, HEAD_DIM).astype(jnp.bfloat16)
        values = packed_columns(LANES + kv_width + head * HEAD_DIM, HEAD_DIM).astype(jnp.bfloat16)
        base = head * group * HEAD_DIM
        own = packed_columns(q_base + base, group * HEAD_DIM).astype(jnp.bfloat16)
        queries = jnp.concatenate(
            [own[:, g * HEAD_DIM : (g + 1) * HEAD_DIM] for g in range(group)], axis=0
        )
        scores = (
            lax.dot_general(queries, keys, (((1,), (1,)), ((), ())), preferred_element_type=jnp.float32)
            * scale
        )
        scores = jnp.where(allowed, scores, BIG_NEG)
        top = jnp.max(scores, axis=1, keepdims=True)
        prob = jnp.exp(scores - top)
        total = jnp.sum(prob, axis=1, keepdims=True)
        mixed = jnp.dot(prob.astype(jnp.bfloat16), values, preferred_element_type=jnp.float32) / total
        for g in range(group):
            attn_ref[:, base + g * HEAD_DIM : base + (g + 1) * HEAD_DIM] = mixed[
                g * packed : (g + 1) * packed
            ]
    rows = packed_columns(x_base, width)
    rows = (rows + attn_ref[...]).astype(jnp.bfloat16).astype(jnp.float32)
    scaled = (rows * gain_ref[...].astype(jnp.float32)).astype(jnp.bfloat16)
    square = jnp.sum(rows * rows, axis=1, keepdims=True)
    half = packed // 2
    coarse = square.astype(jnp.bfloat16).astype(jnp.float32)
    fine = square - coarse
    lane = lax.broadcasted_iota(jnp.int32, (packed, LANES), 1)
    note = jnp.where(lane < 64, coarse, fine).astype(jnp.bfloat16)
    keep_ref[:, 2 * hidden_width :] = note[:half]
    send_ref[:, 2 * hidden_width :] = note[half:]
    tile = 256
    for base, ref in ((0, gate_ref), (hidden_width, up_ref)):
        for at in range(0, hidden_width, tile):
            part = jnp.dot(scaled, ref[:, at : at + tile], preferred_element_type=jnp.float32)
            part = part.astype(jnp.bfloat16)
            keep_ref[:, base + at : base + at + tile] = part[:half]
            send_ref[:, base + at : base + at + tile] = part[half:]


def own_kernel(spread_ref, attn_ref, out_ref):
    attn = attn_ref[...]
    coarse = attn.astype(jnp.bfloat16)
    fine = (attn - coarse.astype(jnp.float32)).astype(jnp.bfloat16)
    spread = spread_ref[:CAP]
    out_ref[...] = jnp.dot(spread, coarse, preferred_element_type=jnp.float32) + jnp.dot(
        spread, fine, preferred_element_type=jnp.float32
    )


def fold_kernel(keep_ref, other_ref, *out_refs):
    rows = out_refs[0].shape[0]
    for at, ref in enumerate(out_refs):
        block = slice(at * rows, (at + 1) * rows)
        ref[...] = (
            keep_ref[block].astype(jnp.float32) + other_ref[block].astype(jnp.float32)
        ).astype(jnp.bfloat16)


def hidden_kernel(mine_ref, other_ref, out_ref):
    hidden_width = out_ref.shape[1]
    square = mine_ref[:, 2 * hidden_width :].astype(jnp.float32) + other_ref[
        :, 2 * hidden_width :
    ].astype(jnp.float32)
    rscale = lax.rsqrt((square[:, :1] + square[:, 64:65]) / D + EPSILON)
    gate = rscale * (
        mine_ref[:, :hidden_width].astype(jnp.float32) + other_ref[:, :hidden_width].astype(jnp.float32)
    )
    up = rscale * (
        mine_ref[:, hidden_width : 2 * hidden_width].astype(jnp.float32)
        + other_ref[:, hidden_width : 2 * hidden_width].astype(jnp.float32)
    )
    out_ref[...] = (gate / (1.0 + jnp.exp(-gate)) * up).astype(jnp.bfloat16)


def down_kernel(hidden_ref, down_ref, spread_ref, keep_ref, send_ref):
    half = keep_ref.shape[0]
    spread = spread_ref[...]
    hidden = hidden_ref[...]
    tile = 256
    for at in range(0, down_ref.shape[1], tile):
        part = jnp.dot(hidden, down_ref[:, at : at + tile], preferred_element_type=jnp.float32)
        out = jnp.dot(spread, part.astype(jnp.bfloat16), preferred_element_type=jnp.float32)
        out = out.astype(jnp.bfloat16)
        keep_ref[:, at : at + tile] = out[:half]
        send_ref[:, at : at + tile] = out[half:]


def finish_kernel(router_ref, load_ref, attn_ref, a_ref, b_ref, c_ref, d_ref, out_ref):
    width = out_ref.shape[1]
    base = load_ref.shape[1] - 2 * width
    mlp = a_ref[...].astype(jnp.float32) + b_ref[...].astype(jnp.float32)
    mlp = mlp + (c_ref[...].astype(jnp.float32) + d_ref[...].astype(jnp.float32))
    mlp = mlp.astype(jnp.bfloat16).astype(jnp.float32)
    rows = load_ref[:, base : base + width].astype(jnp.float32)
    result = rows + router_ref[:, :1] * (attn_ref[...] + mlp)
    out_ref[...] = jnp.where(router_ref[:, 64:65] > 0.5, result, 0.0).astype(jnp.bfloat16)


def run(kernel, name, outs, scalars, loose, arrays, keep_out=True):
    smem = pl.BlockSpec(memory_space=pltpu.SMEM)
    vmem = pl.BlockSpec(memory_space=pltpu.VMEM)
    arrays = list(loose) + [pltpu.with_memory_space_constraint(array, pltpu.VMEM) for array in arrays]
    place = pltpu.VMEM if keep_out else jax.ShapeDtypeStruct
    return pl.pallas_call(
        kernel,
        out_shape=tuple(place(shape, dtype) for shape, dtype in outs),
        in_specs=[smem] * len(scalars) + [vmem] * len(arrays),
        out_specs=(vmem,) * len(outs),
        compiler_params=pltpu.CompilerParams(vmem_limit_bytes=8 << 20),
        name=name,
    )(*scalars, *arrays)


def swap(value, axis, mask):
    pairs = [(source, source ^ mask) for source in range(lax.axis_size(axis))]
    return lax.ppermute(value, axis, pairs)


def gathered(piece):
    across = [piece] + [swap(piece, "ctx", mask) for mask in (2, 4, 6)]
    return across + [swap(part, "ctx", 1) for part in across]


def local(
    resid, query, key, value, router_logit, norm_gain, w_gate, w_up, w_down, sel_index, sel_count
):
    shards = lax.axis_size("ctx")
    tps = lax.axis_size("tp")
    tok_ctx, width = resid.shape
    kv_width = key.shape[1]
    hidden_width = w_gate.shape[1]
    if not fits(shards, tps, tok_ctx, width, kv_width, hidden_width):
        return local_exchange(
            resid, query, key, value, router_logit, norm_gain, w_gate, w_up, w_down, sel_index, sel_count
        )
    slots = shards * CAP
    packed = slots // 2
    half = packed // 2
    quarter = packed // 4
    bf16 = jnp.bfloat16
    f32 = jnp.float32
    place = jnp.stack([lax.axis_index("ctx"), lax.axis_index("tp"), jnp.int32(tok_ctx)]).astype(jnp.int32)
    smem = pl.BlockSpec(memory_space=pltpu.SMEM)
    vmem = pl.BlockSpec(memory_space=pltpu.VMEM)
    hbm = pl.BlockSpec(memory_space=pltpu.HBM)
    load_width = LANES + 2 * kv_width + 2 * width
    sources = [sel_index, router_logit.reshape(1, tok_ctx), resid, query, key, value]
    load, router = pl.pallas_call(
        gather_kernel,
        out_shape=(pltpu.VMEM((CAP, load_width), bf16), pltpu.VMEM((CAP, LANES), f32)),
        in_specs=[smem] + [hbm] * 6,
        out_specs=(vmem,) * 2,
        scratch_shapes=[pltpu.VMEM(source.shape, source.dtype) for source in sources]
        + [pltpu.SemaphoreType.DMA((6,))],
        compiler_params=pltpu.CompilerParams(vmem_limit_bytes=8 << 20),
        name="gather_rows",
    )(sel_count, *[pltpu.with_memory_space_constraint(source, pltpu.HBM) for source in sources])
    wide = 2 * hidden_width + LANES
    keep, send, attn, spread = run(
        mix_kernel,
        "mix",
        [((half, wide), bf16), ((half, wide), bf16), ((packed, width), f32), ((slots, packed), bf16)],
        [place],
        [],
        [*gathered(load), norm_gain.reshape(1, width), w_gate, w_up],
    )
    (own,) = run(own_kernel, "own", [((CAP, width), f32)], [], [], [spread, attn])
    keep, send = run(
        fold_kernel,
        "fold_tp",
        [((quarter, wide), bf16), ((quarter, wide), bf16)],
        [],
        [],
        [keep, swap(send, "tp", 1)],
    )
    (hidden,) = run(
        hidden_kernel,
        "hidden",
        [((quarter, hidden_width), bf16)],
        [],
        [],
        [keep, swap(send, "tp", 2)],
    )
    hidden = jnp.concatenate([hidden, swap(hidden, "tp", 2)], axis=0)
    hidden = jnp.concatenate([hidden, swap(hidden, "tp", 1)], axis=0)
    half = slots // 2
    keep, send = run(
        down_kernel,
        "down",
        [((half, width), bf16), ((half, width), bf16)],
        [],
        [],
        [hidden, w_down, spread],
    )
    pieces = run(
        fold_kernel,
        "fold_ctx",
        [((CAP, width), bf16)] * 4,
        [],
        [],
        [keep, swap(send, "ctx", 1)],
    )
    pieces = [pieces[0]] + [swap(pieces[b], "ctx", 2 * b) for b in range(1, 4)]
    (out,) = run(
        finish_kernel,
        "finish",
        [((CAP, width), bf16)],
        [],
        [],
        [router, load, own, *pieces],
        keep_out=False,
    )
    return out


def solution(mesh):
    in_specs = (
        P("ctx", "tp"),
        P("ctx", "tp"),
        P("ctx", "tp"),
        P("ctx", "tp"),
        P("ctx"),
        P("tp"),
        P("tp", "ctx"),
        P("tp", "ctx"),
        P("ctx", "tp"),
        P("ctx", None),
        P("ctx"),
    )
    out_specs = P("ctx", "tp")
    return jax.shard_map(local, mesh=mesh, in_specs=in_specs, out_specs=out_specs, check_vma=False)
```

```python
import jax
import jax.numpy as jnp
from jax import lax
from jax.experimental import pallas as pl
from jax.experimental.pallas import tpu as pltpu
from jax.sharding import PartitionSpec as P


D = 4096
HEAD_DIM = 128
CAP = 32


BIG_NEG = -1e30
EPSILON = 1e-05


def swapped(value, axis, distance):
    mask = 2**distance
    pairs = [(source, source ^ mask) for source in range(lax.axis_size(axis))]
    return lax.ppermute(value, axis, pairs)


def masked_scores(queries, keys, key_pos, query_pos, scale):
    scores = jnp.einsum("qkgd,skd->kgqs", queries, keys, preferred_element_type=jnp.float32) * scale
    allowed = key_pos[None, :] <= query_pos[:, None]
    return jnp.where(allowed[None, None], scores, BIG_NEG)


def pick_bit(shard_index, bit):
    return shard_index // (1 << bit) % 2


def ordered(own_piece, partner_piece, my_bit, along):
    lower_part = jnp.where(my_bit == 0, own_piece, partner_piece)
    upper_part = jnp.where(my_bit == 0, partner_piece, own_piece)
    return jnp.concatenate([lower_part, upper_part], axis=along)


def route_members(blocks, low_bits, my_shard, mover):
    per_dest = blocks.shape[1]
    width = blocks.shape[2]
    blocks_now = blocks.reshape((2,) * low_bits + (per_dest, width))
    for bit in range(low_bits):
        my_bit = pick_bit(my_shard, bit)
        retained = lax.dynamic_index_in_dim(blocks_now, my_bit, low_bits - 1, keepdims=False)
        outgoing = lax.dynamic_index_in_dim(blocks_now, 1 - my_bit, low_bits - 1, keepdims=False)
        arrived = mover(outgoing, bit)
        lower_part = jnp.where(my_bit == 0, retained, arrived)
        upper_part = jnp.where(my_bit == 0, arrived, retained)
        blocks_now = jnp.stack([lower_part, upper_part], axis=0)
    return blocks_now.reshape(blocks.shape)


def local_exchange(
    resid, query, key, value, router_logit, norm_gain, w_gate, w_up, w_down, sel_index, sel_count
):
    shards = lax.axis_size("ctx")
    my_shard = lax.axis_index("ctx")
    tok_ctx = resid.shape[0]
    width = resid.shape[1]
    kv_local = key.shape[1] // HEAD_DIM
    group = query.shape[1] // key.shape[1]
    scale = HEAD_DIM ** (-0.5)
    index = sel_index[0]
    count = sel_count[0]
    slot = jnp.arange(CAP, dtype=jnp.int32)
    live = slot < count
    query_pos = my_shard * tok_ctx + index
    key_pos = jnp.where(live, query_pos, tok_ctx * shards)
    rows_x = jnp.take(resid, index, axis=0)
    q_rows = jnp.take(query, index, axis=0).reshape(CAP, kv_local, group, HEAD_DIM)
    k_rows = jnp.take(key, index, axis=0)
    v_rows = jnp.take(value, index, axis=0)
    router = jax.nn.sigmoid(jnp.take(router_logit, index, axis=0))
    all_k, all_v, all_pos = (
        lax.all_gather(k_rows, "ctx", axis=0, tiled=True),
        lax.all_gather(v_rows, "ctx", axis=0, tiled=True),
        lax.all_gather(key_pos, "ctx", axis=0, tiled=True),
    )
    scores = masked_scores(q_rows, all_k.reshape(-1, kv_local, HEAD_DIM), all_pos, query_pos, scale)
    top = jnp.max(scores, axis=-1, keepdims=True)
    prob = jnp.exp(scores - top)
    total = jnp.sum(prob, axis=-1)
    mixed = jnp.einsum(
        "kgqs,skd->kgqd",
        prob.astype(jnp.bfloat16),
        all_v.reshape(-1, kv_local, HEAD_DIM),
        preferred_element_type=jnp.float32,
    )
    mixed = mixed / total[..., None]
    attn = mixed.transpose(2, 0, 1, 3).reshape(CAP, width)
    rows_float = rows_x.astype(jnp.float32)
    h_one = (rows_float + attn).astype(jnp.bfloat16)
    low_bits = 2
    members = 1 << low_bits
    high_bits = shards.bit_length() - 1 - low_bits
    per_dest = CAP // members
    weight_pair = jnp.stack([w_gate, w_up], axis=0)
    down_block = w_down
    for bit in range(low_bits):
        my_bit = pick_bit(my_shard, bit)
        weight_pair = ordered(weight_pair, swapped(weight_pair, "ctx", bit), my_bit, 2)
        down_block = ordered(down_block, swapped(down_block, "ctx", bit), my_bit, 0)

    def send_rows(piece, bit):
        return swapped(piece, "ctx", bit)

    def send_back(piece, bit):
        return swapped(piece, "ctx", bit)

    routed = route_members(h_one.reshape(members, per_dest, width), low_bits, my_shard, send_rows)
    spread = routed.reshape(members * per_dest, width)
    for step in range(high_bits):
        bit = low_bits + step
        spread = ordered(spread, swapped(spread, "ctx", bit), pick_bit(my_shard, bit), 0)
    compact_float = spread.astype(jnp.float32)
    square_part = jnp.sum(compact_float * compact_float, axis=1)
    scaled = (compact_float * norm_gain.astype(jnp.float32)[None, :]).astype(jnp.bfloat16)
    gate_part = jnp.dot(scaled, weight_pair[0], preferred_element_type=jnp.float32)
    up_part = jnp.dot(scaled, weight_pair[1], preferred_element_type=jnp.float32)
    gate_sum, up_sum, square_sum = lax.psum((gate_part, up_part, square_part), "tp")
    rscale = lax.rsqrt(square_sum / D + EPSILON)
    hidden = (jax.nn.silu(rscale[:, None] * gate_sum) * (rscale[:, None] * up_sum)).astype(
        jnp.bfloat16
    )
    partial_value = jnp.dot(hidden, down_block, preferred_element_type=jnp.float32)
    partial_value = partial_value.reshape(1 << high_bits, members * per_dest, width)
    for step in reversed(range(high_bits)):
        bit = low_bits + step
        my_bit = pick_bit(my_shard, bit)
        halves = partial_value.reshape(2, partial_value.shape[0] // 2, members * per_dest, width)
        retained = lax.dynamic_index_in_dim(halves, my_bit, 0, keepdims=False)
        outgoing = lax.dynamic_index_in_dim(halves, 1 - my_bit, 0, keepdims=False)
        partial_value = retained + swapped(outgoing, "ctx", bit)
    mlp_rows = partial_value[0].astype(jnp.bfloat16).reshape(members, per_dest, width)
    mine = route_members(mlp_rows, low_bits, my_shard, send_back).reshape(CAP, width)
    result = rows_float + router[:, None] * (attn + mine.astype(jnp.float32))
    return jnp.where(live[:, None], result, 0.0).astype(jnp.bfloat16)


LANES = 128
ROWS = 32


def fits(shards, tps, tok_ctx, width, kv_width, hidden_width):
    return (
        shards == 8
        and tps == 4
        and tok_ctx % LANES == 0
        and width % LANES == 0
        and kv_width % HEAD_DIM == 0
        and hidden_width % 256 == 0
    )


def block_shard(block, my_shard):
    return my_shard ^ (((block & 3) << 1) | (block >> 2))


def column_of(row, size):
    down = lax.broadcasted_iota(jnp.int32, (size, size), 0)
    across = lax.broadcasted_iota(jnp.int32, (size, size), 1)
    return jnp.sum(jnp.where(down == across, row, jnp.zeros_like(row)), axis=1, keepdims=True)


def row_of(column, size):
    down = lax.broadcasted_iota(jnp.int32, (size, size), 0)
    across = lax.broadcasted_iota(jnp.int32, (size, size), 1)
    return jnp.sum(jnp.where(down == across, column, jnp.zeros_like(column)), axis=0, keepdims=True)


def gather_kernel(
    place_ref,
    count_ref,
    index_hbm,
    logit_hbm,
    resid_hbm,
    query_hbm,
    key_hbm,
    value_hbm,
    load_ref,
    first_ref,
    last_ref,
    router_ref,
    index_ref,
    logit_ref,
    resid_ref,
    query_ref,
    key_ref,
    value_ref,
    sems,
):
    sources = (index_hbm, key_hbm, value_hbm, resid_hbm, query_hbm, logit_hbm)
    places = (index_ref, key_ref, value_ref, resid_ref, query_ref, logit_ref)
    copies = [
        pltpu.make_async_copy(source, target, sems.at[at])
        for at, (source, target) in enumerate(zip(sources, places))
    ]
    for copy in copies:
        copy.start()
    tok_ctx = resid_ref.shape[0]
    kv_width = key_ref.shape[1]
    width = resid_ref.shape[1]
    copies[0].wait()
    index = column_of(index_ref[...], CAP)
    chosen = lax.broadcasted_iota(jnp.int32, (CAP, tok_ctx), 1) == index
    pick = chosen.astype(jnp.bfloat16)

    def take(at, base):
        copies[at].wait()
        rows = jnp.dot(pick, places[at][...], preferred_element_type=jnp.float32)
        load_ref[:, base : base + rows.shape[1]] = rows.astype(jnp.bfloat16)

    lane = lax.broadcasted_iota(jnp.int32, (CAP, LANES), 1)
    live = (lax.broadcasted_iota(jnp.int32, (CAP, LANES), 0) < count_ref[0]).astype(jnp.int32)
    position = place_ref[0] * tok_ctx + index
    note = jnp.where(lane < 32, position % LANES, jnp.where(lane < 64, position // LANES, live))
    load_ref[:, :LANES] = note.astype(jnp.float32).astype(jnp.bfloat16)
    take(1, LANES)
    take(2, LANES + kv_width)
    take(4, LANES + 2 * kv_width)
    take(3, LANES + 2 * kv_width + width)
    first_ref[...] = load_ref[:, : first_ref.shape[1]]
    last_ref[...] = load_ref[:, first_ref.shape[1] :]
    copies[5].wait()
    logit = jnp.sum(jnp.where(chosen, logit_ref[...], 0.0), axis=1, keepdims=True)
    router = 1.0 / (1.0 + jnp.exp(-logit))
    router_ref[...] = jnp.where(lane < 64, router, live.astype(jnp.float32))


def attend_kernel(place_ref, *refs):
    loads = refs[:8]
    attn_ref, pack_ref, spread_ref = refs[8:]
    my_shard = place_ref[0]
    my_tp = place_ref[1]
    slots = spread_ref.shape[0]
    packed = spread_ref.shape[1]
    width = attn_ref.shape[1]
    kv_width = (loads[-1].shape[1] - LANES - width) // 2
    kv_heads = kv_width // HEAD_DIM
    group = width // kv_width
    scale = HEAD_DIM ** (-0.5)

    notes = jnp.concatenate([ref[:, :LANES] for ref in loads], axis=0).astype(jnp.float32)
    live = notes[:, 64:65]
    down = lax.broadcasted_iota(jnp.int32, (slots, slots), 0)
    across = lax.broadcasted_iota(jnp.int32, (slots, slots), 1)

    def order(slot):
        return block_shard(slot // CAP, my_shard) * CAP + slot % CAP

    before = (order(across) < order(down)).astype(jnp.float32)
    place = jnp.sum(before * row_of(live, slots), axis=1, keepdims=True).astype(jnp.int32)
    relative = (place // ROWS) ^ my_tp
    swapped_bits = ((relative & 1) << 1) | (relative >> 1)
    spot = jnp.where(live > 0.5, swapped_bits * ROWS + place % ROWS, packed).astype(jnp.float32)
    spread_ref[...] = (
        lax.broadcasted_iota(jnp.int32, (slots, packed), 1).astype(jnp.float32) == spot
    ).astype(jnp.bfloat16)
    hit = lax.broadcasted_iota(jnp.int32, (packed, slots), 0).astype(jnp.float32) == row_of(spot, slots)
    pack = hit.astype(jnp.bfloat16)
    pack_ref[...] = pack
    position = notes[:, :1] + LANES * notes[:, 32:33]
    position = jnp.sum(jnp.where(hit, row_of(position, slots), 0.0), axis=1, keepdims=True)
    allowed = row_of(position, packed) <= position
    allowed = jnp.concatenate([allowed] * group, axis=0)

    def packed_columns(base, size):
        rows = jnp.concatenate([ref[:, base : base + size] for ref in loads], axis=0)
        return jnp.dot(pack, rows, preferred_element_type=jnp.float32).astype(jnp.bfloat16)

    q_base = LANES + 2 * kv_width
    for head in range(kv_heads):
        keys = packed_columns(LANES + head * HEAD_DIM, HEAD_DIM)
        values = packed_columns(LANES + kv_width + head * HEAD_DIM, HEAD_DIM)
        base = head * group * HEAD_DIM
        own = packed_columns(q_base + base, group * HEAD_DIM)
        queries = jnp.concatenate(
            [own[:, g * HEAD_DIM : (g + 1) * HEAD_DIM] for g in range(group)], axis=0
        )
        scores = (
            lax.dot_general(queries, keys, (((1,), (1,)), ((), ())), preferred_element_type=jnp.float32)
            * scale
        )
        scores = jnp.where(allowed, scores, BIG_NEG)
        top = jnp.max(scores, axis=1, keepdims=True)
        prob = jnp.exp(scores - top)
        total = jnp.sum(prob, axis=1, keepdims=True)
        mixed = jnp.dot(prob.astype(jnp.bfloat16), values, preferred_element_type=jnp.float32) / total
        for g in range(group):
            attn_ref[:, base + g * HEAD_DIM : base + (g + 1) * HEAD_DIM] = mixed[
                g * packed : (g + 1) * packed
            ]


def expand_kernel(*refs):
    loads = refs[:8]
    pack_ref, attn_ref, gain_ref, gate_ref, up_ref, keep_ref, send_ref = refs[8:]
    packed, width = attn_ref.shape
    hidden_width = gate_ref.shape[1]
    rows = jnp.concatenate([ref[:, ref.shape[1] - width :] for ref in loads], axis=0)
    rows = jnp.dot(pack_ref[...], rows, preferred_element_type=jnp.float32)
    rows = (rows + attn_ref[...]).astype(jnp.bfloat16).astype(jnp.float32)
    scaled = (rows * gain_ref[...].astype(jnp.float32)).astype(jnp.bfloat16)
    square = jnp.sum(rows * rows, axis=1, keepdims=True)
    half = packed // 2
    coarse = square.astype(jnp.bfloat16).astype(jnp.float32)
    fine = square - coarse
    lane = lax.broadcasted_iota(jnp.int32, (packed, LANES), 1)
    note = jnp.where(lane < 64, coarse, fine).astype(jnp.bfloat16)
    keep_ref[:, 2 * hidden_width :] = note[:half]
    send_ref[:, 2 * hidden_width :] = note[half:]
    tile = 256
    for base, ref in ((0, gate_ref), (hidden_width, up_ref)):
        for at in range(0, hidden_width, tile):
            part = jnp.dot(scaled, ref[:, at : at + tile], preferred_element_type=jnp.float32)
            part = part.astype(jnp.bfloat16)
            keep_ref[:, base + at : base + at + tile] = part[:half]
            send_ref[:, base + at : base + at + tile] = part[half:]


def stage_kernel(*refs):
    count = (len(refs) - 1) // 2
    sems = refs[-1]
    copies = [
        pltpu.make_async_copy(refs[at], refs[count + at], sems.at[at]) for at in range(count)
    ]
    for copy in copies:
        copy.start()
    for copy in copies:
        copy.wait()


def staged(*arrays):
    hbm = pl.BlockSpec(memory_space=pltpu.HBM)
    vmem = pl.BlockSpec(memory_space=pltpu.VMEM)
    return pl.pallas_call(
        stage_kernel,
        out_shape=tuple(pltpu.VMEM(array.shape, array.dtype) for array in arrays),
        in_specs=[hbm] * len(arrays),
        out_specs=(vmem,) * len(arrays),
        scratch_shapes=[pltpu.SemaphoreType.DMA((len(arrays),))],
        compiler_params=pltpu.CompilerParams(vmem_limit_bytes=1 << 20),
    )(*[pltpu.with_memory_space_constraint(array, pltpu.HBM) for array in arrays])


def own_kernel(spread_ref, attn_ref, out_ref):
    attn = attn_ref[...]
    coarse = attn.astype(jnp.bfloat16)
    fine = (attn - coarse.astype(jnp.float32)).astype(jnp.bfloat16)
    spread = spread_ref[:CAP]
    out_ref[...] = jnp.dot(spread, coarse, preferred_element_type=jnp.float32) + jnp.dot(
        spread, fine, preferred_element_type=jnp.float32
    )


def fold_kernel(keep_ref, other_ref, *out_refs):
    rows = out_refs[0].shape[0]
    for at, ref in enumerate(out_refs):
        block = slice(at * rows, (at + 1) * rows)
        ref[...] = (
            keep_ref[block].astype(jnp.float32) + other_ref[block].astype(jnp.float32)
        ).astype(jnp.bfloat16)


def hidden_kernel(mine_ref, other_ref, out_ref):
    hidden_width = out_ref.shape[1]
    square = mine_ref[:, 2 * hidden_width :].astype(jnp.float32) + other_ref[
        :, 2 * hidden_width :
    ].astype(jnp.float32)
    rscale = lax.rsqrt((square[:, :1] + square[:, 64:65]) / D + EPSILON)
    gate = rscale * (
        mine_ref[:, :hidden_width].astype(jnp.float32) + other_ref[:, :hidden_width].astype(jnp.float32)
    )
    up = rscale * (
        mine_ref[:, hidden_width : 2 * hidden_width].astype(jnp.float32)
        + other_ref[:, hidden_width : 2 * hidden_width].astype(jnp.float32)
    )
    out_ref[...] = (gate / (1.0 + jnp.exp(-gate)) * up).astype(jnp.bfloat16)


def down_kernel(hidden_ref, down_ref, spread_ref, *out_refs):
    rows = out_refs[0].shape[0]
    spread = spread_ref[...]
    hidden = hidden_ref[...]
    tile = 256
    for at in range(0, down_ref.shape[1], tile):
        part = jnp.dot(hidden, down_ref[:, at : at + tile], preferred_element_type=jnp.float32)
        out = jnp.dot(spread, part.astype(jnp.bfloat16), preferred_element_type=jnp.float32)
        out = out.astype(jnp.bfloat16)
        for block, ref in enumerate(out_refs):
            ref[:, at : at + tile] = out[block * rows : (block + 1) * rows]


def finish_kernel(router_ref, load_ref, attn_ref, a_ref, b_ref, c_ref, d_ref, out_ref):
    width = out_ref.shape[1]
    base = load_ref.shape[1] - width
    mlp = a_ref[...].astype(jnp.float32) + b_ref[...].astype(jnp.float32)
    mlp = mlp + (c_ref[...].astype(jnp.float32) + d_ref[...].astype(jnp.float32))
    mlp = mlp.astype(jnp.bfloat16).astype(jnp.float32)
    rows = load_ref[:, base : base + width].astype(jnp.float32)
    result = rows + router_ref[:, :1] * (attn_ref[...] + mlp)
    out_ref[...] = jnp.where(router_ref[:, 64:65] > 0.5, result, 0.0).astype(jnp.bfloat16)


def run(kernel, outs, scalars, loose, arrays, fetched=(), keep_out=True):
    smem = pl.BlockSpec(memory_space=pltpu.SMEM)
    vmem = pl.BlockSpec(memory_space=pltpu.VMEM)
    hbm = pl.BlockSpec(memory_space=pltpu.HBM)
    arrays = list(loose) + [pltpu.with_memory_space_constraint(array, pltpu.VMEM) for array in arrays]
    weights = [pltpu.with_memory_space_constraint(array, pltpu.HBM) for array in fetched]
    scratch = [pltpu.VMEM(array.shape, array.dtype) for array in fetched]
    if fetched:
        scratch.append(pltpu.SemaphoreType.DMA((len(fetched),)))
    place = pltpu.VMEM if keep_out else jax.ShapeDtypeStruct
    return pl.pallas_call(
        kernel,
        out_shape=tuple(place(shape, dtype) for shape, dtype in outs),
        in_specs=[smem] * len(scalars) + [vmem] * len(arrays) + [hbm] * len(weights),
        out_specs=(vmem,) * len(outs),
        scratch_shapes=scratch,
        compiler_params=pltpu.CompilerParams(vmem_limit_bytes=(20 if fetched else 8) << 20),
    )(*scalars, *arrays, *weights)


def swap(value, axis, mask):
    pairs = [(source, source ^ mask) for source in range(lax.axis_size(axis))]
    return lax.ppermute(value, axis, pairs)


def gathered(load, first, last):
    across = [load] + [swap(load, "ctx", mask) for mask in (2, 4)]
    nearby = [swap(part, "ctx", 1) for part in across]
    ends = []
    for part in (first, last):
        far = swap(part, "ctx", 6)
        near = swap(far, "ctx", 1)
        ends.append(across + [far] + nearby + [near])
    return ends


def fast(
    resid, query, key, value, router_logit, norm_gain, w_gate, w_up, w_down, sel_index, sel_count
):
    shards = lax.axis_size("ctx")
    tok_ctx, width = resid.shape
    kv_width = key.shape[1]
    hidden_width = w_gate.shape[1]
    slots = shards * CAP
    packed = slots // 2
    half = packed // 2
    quarter = packed // 4
    bf16 = jnp.bfloat16
    f32 = jnp.float32
    place = jnp.stack([lax.axis_index("ctx"), lax.axis_index("tp")]).astype(jnp.int32)
    smem = pl.BlockSpec(memory_space=pltpu.SMEM)
    vmem = pl.BlockSpec(memory_space=pltpu.VMEM)
    hbm = pl.BlockSpec(memory_space=pltpu.HBM)
    load_width = LANES + 2 * kv_width + 2 * width
    sources = [sel_index, router_logit.reshape(1, tok_ctx), resid, query, key, value]
    load, first, last, router = pl.pallas_call(
        gather_kernel,
        out_shape=(
            pltpu.VMEM((CAP, load_width), bf16),
            pltpu.VMEM((CAP, load_width - width), bf16),
            pltpu.VMEM((CAP, width), bf16),
            pltpu.VMEM((CAP, LANES), f32),
        ),
        in_specs=[smem] * 2 + [hbm] * 6,
        out_specs=(vmem,) * 4,
        scratch_shapes=[pltpu.VMEM(source.shape, source.dtype) for source in sources]
        + [pltpu.SemaphoreType.DMA((6,))],
        compiler_params=pltpu.CompilerParams(vmem_limit_bytes=8 << 20),
        name="gather_rows",
    )(place, sel_count, *[pltpu.with_memory_space_constraint(source, pltpu.HBM) for source in sources])
    wide = 2 * hidden_width + LANES
    firsts, lasts = gathered(load, first, last)
    attn, pack, spread = run(
        attend_kernel,
        [((packed, width), f32), ((packed, slots), bf16), ((slots, packed), bf16)],
        [place],
        [],
        firsts,
    )
    keep, send = run(
        expand_kernel,
        [((half, wide), bf16), ((half, wide), bf16)],
        [],
        [],
        [*lasts, pack, attn, norm_gain.reshape(1, width), *staged(w_gate, w_up)],
    )
    (own,) = run(own_kernel, [((CAP, width), f32)], [], [], [spread, attn])
    keep, send = run(
        fold_kernel,
        [((quarter, wide), bf16), ((quarter, wide), bf16)],
        [],
        [],
        [keep, swap(send, "tp", 1)],
    )
    (hidden,) = run(
        hidden_kernel, [((quarter, hidden_width), bf16)], [], [], [keep, swap(send, "tp", 2)]
    )
    hidden = jnp.concatenate([hidden, swap(hidden, "tp", 2)], axis=0)
    hidden = jnp.concatenate([hidden, swap(hidden, "tp", 1)], axis=0)
    quads = run(down_kernel, [((slots // 4, width), bf16)] * 4, [], [], [hidden, w_down, spread])
    pieces = [None] * 4
    for at in (1, 0):
        other = swap(quads[2 + at], "ctx", 1)
        pair = run(fold_kernel, [((CAP, width), bf16)] * 2, [], [], [quads[at], other])
        pieces[2 * at : 2 * at + 2] = pair
    pieces = [pieces[0]] + [swap(pieces[b], "ctx", 2 * b) for b in (1, 2, 3)]
    (out,) = run(
        finish_kernel, [((CAP, width), bf16)], [], [], [router, load, own, *pieces], keep_out=False
    )
    return out


def local(
    resid, query, key, value, router_logit, norm_gain, w_gate, w_up, w_down, sel_index, sel_count
):
    shards = lax.axis_size("ctx")
    tps = lax.axis_size("tp")
    tok_ctx, width = resid.shape
    kv_width = key.shape[1]
    hidden_width = w_gate.shape[1]
    if not fits(shards, tps, tok_ctx, width, kv_width, hidden_width):
        return local_exchange(
            resid, query, key, value, router_logit, norm_gain, w_gate, w_up, w_down, sel_index, sel_count
        )
    return fast(
        resid, query, key, value, router_logit, norm_gain, w_gate, w_up, w_down, sel_index, sel_count
    )


def solution(mesh):
    in_specs = (
        P("ctx", "tp"),
        P("ctx", "tp"),
        P("ctx", "tp"),
        P("ctx", "tp"),
        P("ctx"),
        P("tp"),
        P("tp", "ctx"),
        P("tp", "ctx"),
        P("ctx", "tp"),
        P("ctx", None),
        P("ctx"),
    )
    out_specs = P("ctx", "tp")
    return jax.shard_map(local, mesh=mesh, in_specs=in_specs, out_specs=out_specs, check_vma=False)
```
